32 devices in a mesh: groups: 2 (over y), dp: 4 (over z), tensor: 4 (over x, core).
Axes of the slice: x: 2, y: 2, z: 4, core: 2. Of those that a mesh axis runs over, the one named last changes fastest.
Arguments:
- activations: bfloat16 [4, 512, 8192], P('dp', 'groups', 'tensor'), parts along dimension 1, may hold values from -6 to 6
- out_grads: bfloat16 [4, 512, 28672], P('dp', 'groups', 'tensor'), parts along dimension 1, may hold values from -6 to 6
- lengths: int32 [8], P(('groups', 'dp')), parts along dimension 0, may hold values from 32 to 256, as said below
- query_left: bfloat16 [32, 32, 8192], P(None, 'groups', 'dp'), parts along dimension 1, may hold values from -0.0625 to 0.0625
- query_right: bfloat16 [32, 32, 28672], P('dp', 'groups', 'tensor'), parts along dimension 1, may hold values from -0.03125 to 0.03125
Outputs:
- scores: float32 [4, 32], P('dp', 'groups'), parts along dimension 1
The draws below stay inside these ranges and needn't reach their ends.
There are 2 independent parts, one for each index of `groups`. The reference program is written for one: setup_inputs(seed, part) draws one part's arguments, and reference() takes and returns one part's arrays. A program takes and returns all parts, laid end to end along the dimension named above; each array names one. Nothing has to cross between parts.
Inputs may be any that keep to these rules, and one draw needn't show every extreme that they name: `lengths`: each training sequence's count of valid leading tokens; some sequence has all 256 valid.
All inputs are finite; a program needn't handle non-finite values.
Results may differ from the reference program's by a relative error of at most 0.0003.
Values may be sent and summed in bfloat16 or wider, within the bound.
No kernel may reach another device: no remote copies, remote signals or barrier semaphores. Data moves between devices by JAX's collectives and lax.ppermute only.
A program may use at most 64 MiB of HBM per device.

```python
import functools
import math
import jax
import jax.numpy as jnp
from jax import lax

D = 8192
FF = 28672
RANK = 32
QRY = 16
LEN = 256
SEQS = 4


def draw_lengths(key, part):
    counts = jax.random.randint(key, (SEQS,), LEN // 8, LEN + 1, dtype=jnp.int32)
    return counts.at[0].set(LEN)


def level_of(key, extent, pieces, least, top_value):
    level, own = 1.0, jax.random.fold_in(key, 6)
    for position, parts in pieces:
        steps = jnp.exp(jax.random.uniform(jax.random.fold_in(own, position), (parts,), jnp.float32, least / len(pieces), top_value / len(pieces)))
        level = level * jnp.repeat(steps, extent[position] // parts).reshape([-1 if axis == position else 1 for axis in range(len(extent))])
    return level


def gaussian(own_key, shape, scale, limit, cuts=(), kind=jnp.bfloat16):
    values = scale * jax.random.normal(own_key, shape, jnp.float32)
    if cuts:
        values = values * level_of(own_key, shape, cuts, -0.22, 0.18)
    return jnp.clip(values, -limit, limit).astype(kind)


def setup_inputs(seed: int = 0, part: int = 0) -> dict:
    key_list = jax.random.split(jax.random.key(seed), 6)
    part_keys = jax.random.split(jax.random.fold_in(key_list[5], part), 6)
    activations = gaussian(part_keys[0], (SEQS, LEN, D), 1.0, 6.0, ((0, 4), (2, 4)))
    out_grads = gaussian(part_keys[1], (SEQS, LEN, FF), 1.0, 6.0, ((0, 4), (2, 4)))
    lengths = draw_lengths(jax.random.fold_in(jax.random.fold_in(key_list[5], part), 71), part)
    query_left = gaussian(part_keys[3], (RANK, QRY, D), D ** -0.5, 0.0625, ((2, 4),))
    query_right = gaussian(part_keys[4], (RANK, QRY, FF), FF ** -0.5, 0.03125, ((0, 4), (2, 4)))
    return {"activations": activations, "out_grads": out_grads, "lengths": lengths, "query_left": query_left, "query_right": query_right}


def one_sequence(left_flat, right_flat, sequence_item):
    rows_act, rows_grad, valid_count = sequence_item
    left_proj = jnp.dot(rows_act, left_flat.T, preferred_element_type=jnp.float32)
    right_proj = jnp.dot(rows_grad, right_flat.T, preferred_element_type=jnp.float32)
    valid_rows = (lax.broadcasted_iota(jnp.int32, (LEN, 1), 0) < valid_count).astype(jnp.float32)
    summed = lax.optimization_barrier(jnp.sum(left_proj * right_proj * valid_rows, axis=0)).reshape(RANK, QRY)
    return lax.optimization_barrier(jnp.sum(summed, axis=0)) / math.sqrt(LEN * RANK)

def reference(activations, out_grads, lengths, query_left, query_right):
    left_flat = query_left.reshape(RANK * QRY, D)
    right_flat = query_right.reshape(RANK * QRY, FF)
    scorer = functools.partial(one_sequence, left_flat, right_flat)
    return lax.map(scorer, (activations, out_grads, lengths))
```

```python
import math

import jax
import jax.numpy as jnp
from jax import lax
from jax.sharding import PartitionSpec as P

RANK = 32

EDGE = [(0, 1), (1, 0), (2, 3), (3, 2)]
INWARD = [(0, 1), (3, 2)]
OUTWARD = [(1, 0), (2, 3)]
MIDDLE = [(1, 2), (2, 1)]


def after(value, *earlier):
    return lax.optimization_barrier((value, *earlier))[0]


def dot_t(a, b):
    return lax.dot_general(a, b, (((1,), (1,)), ((), ())), preferred_element_type=jnp.float32)


def line_shards(activations, out_grads, lengths, query_left, query_right):
    seq_len = activations.shape[1]
    act = activations.reshape(seq_len, activations.shape[2])
    grad = out_grads.reshape(seq_len, out_grads.shape[2])
    rank_count = RANK
    query_count = query_left.shape[1]
    lanes = lax.axis_size("tensor")
    node = lax.axis_index("dp")
    lane = lax.axis_index("tensor")
    left_rows = query_left.reshape(rank_count * query_count, query_left.shape[2])
    block = query_right.shape[0] * query_count
    right_rows = query_right.reshape(block, query_right.shape[2])
    width = right_rows.shape[1]
    piece = width // 7
    cut1, cut2 = 2 * piece, 4 * piece
    share = left_rows.shape[1] // lanes

    def hop(value, pairs):
        return lax.ppermute(value, "dp", pairs)

    def swap(value, distance):
        return lax.ppermute(value, "tensor", [(k, k ^ distance) for k in range(lanes)])

    def part(value, index):
        return lax.dynamic_slice_in_dim(value, index * share, share, 1)

    left_own = part(left_rows, lane)
    y1_own = right_rows[:, :cut1]
    y2_own = right_rows[:, cut1:cut2]
    x_own = right_rows[:, cut2:]

    left_edge = hop(left_own, EDGE)
    left_mid = hop(left_own, MIDDLE)
    y1_edge = hop(y1_own, EDGE)
    y1_mid = hop(y1_own, MIDDLE)
    left_far = hop(left_edge, MIDDLE)
    left_out = hop(left_mid, OUTWARD)
    y2_own_b = after(y2_own, left_edge, left_mid)
    y2_edge = hop(y2_own_b, EDGE)
    y2_mid = hop(after(y2_own_b, y1_mid), MIDDLE)
    x_own_b = after(x_own, y1_edge)
    x_edge = hop(x_own_b, INWARD)
    left_outfar = hop(left_far, OUTWARD)
    x_mid = hop(after(x_own_b, left_far), MIDDLE)
    y1_out = hop(after(y1_mid, y2_edge), OUTWARD)
    grad_x = grad[:, cut2:]
    grad_edge = hop(after(grad_x, y2_edge), INWARD)
    y1_far = hop(after(y1_edge, y2_mid), MIDDLE)
    y2_out = hop(after(y2_mid, left_outfar), OUTWARD)
    y2_far = hop(after(y2_edge, x_mid), MIDDLE)
    y1_outfar = hop(after(y1_far, y1_out), OUTWARD)
    x_far = hop(after(x_edge, y1_far), MIDDLE)
    y2_outfar = hop(after(y2_far, y2_out), OUTWARD)

    acts = [part(act, lane)]
    for k in range(1, lanes):
        acts.append(swap(after(part(act, lane ^ k), left_edge), k))
    acts = jnp.stack(acts)
    third = jnp.where(node < 2, 2, 1)
    fourth = jnp.where(node < 2, 3, 0)
    order = (node, node ^ 1, third, fourth)
    lefts = (left_own, left_edge, left_mid + left_out, left_far + left_outfar)
    left = 0.0
    for position, rows in zip(order, lefts):
        mine = lax.dynamic_index_in_dim(acts, position ^ lane, 0, keepdims=False)
        left = left + dot_t(mine, rows)
    distance = 1
    while distance < lanes:
        left = left + swap(left, distance)
        distance *= 2
    valid_rows = (lax.broadcasted_iota(jnp.int32, (seq_len, 1), 0) < lengths[0]).astype(jnp.float32)
    left = left * valid_rows
    left_end = hop(left, INWARD)

    is_mid = jnp.logical_or(node == 1, node == 2).astype(jnp.float32)
    left_both = jnp.concatenate([left * is_mid, left_end], axis=0)
    grad_both = jnp.concatenate([grad_x, grad_edge], axis=0)
    y1s = (y1_own, y1_edge, y1_mid + y1_out, y1_far + y1_outfar)
    y2s = (y2_own, y2_edge, y2_mid + y2_out, y2_far + y2_outfar)
    xs = (x_own, x_edge, x_mid, x_far)
    own = jnp.zeros((block,), jnp.float32)
    end = jnp.zeros((block,), jnp.float32)
    for position, y1, y2, x in zip(order, y1s, y2s, xs):
        right_y = dot_t(grad[:, :cut1], y1) + dot_t(grad[:, cut1:cut2], y2)
        right_x = dot_t(grad_both, x)
        columns = lax.dynamic_slice_in_dim(left, position * block, block, 1)
        columns_both = lax.dynamic_slice_in_dim(left_both, position * block, block, 1)
        own = own + jnp.sum(columns * right_y, axis=0)
        product = columns_both * right_x
        own = own + jnp.sum(product[:seq_len], axis=0)
        end = end + jnp.sum(product[seq_len:], axis=0)

    def per_query(value):
        return jnp.sum(value.reshape(block // query_count, query_count), axis=0)[None]

    slot = lax.broadcasted_iota(jnp.int32, (4, 1), 0)
    table = jnp.where(slot == node, per_query(own), 0.0) + jnp.where(
        slot == node ^ 1, per_query(end), 0.0
    )
    table = lax.psum(table / math.sqrt(seq_len * rank_count), ("dp", "tensor"))
    return lax.dynamic_slice_in_dim(table, node, 1, 0)


def gather_shards(activations, out_grads, lengths, query_left, query_right):
    seq_len = activations.shape[1]
    act_rows = activations.reshape(seq_len, activations.shape[2])
    grad_rows = out_grads.reshape(seq_len, out_grads.shape[2])
    rank_count = RANK
    query_count = query_left.shape[1]
    shard_piece = lax.all_gather(query_right, "dp", axis=0, tiled=True)
    flat_piece = shard_piece.reshape(shard_piece.shape[0] * query_count, shard_piece.shape[2])
    right_proj = dot_t(grad_rows, flat_piece)
    rank_blocks = lax.all_to_all(query_left, "dp", split_axis=0, concat_axis=2, tiled=True)
    slice_width = act_rows.shape[1]
    offset = lax.axis_index("tensor") * slice_width
    own_columns = lax.dynamic_slice_in_dim(rank_blocks, offset, slice_width, 2)
    shard_piece = lax.all_gather(own_columns, "dp", axis=0, tiled=True)
    flat_piece = shard_piece.reshape(shard_piece.shape[0] * query_count, slice_width)
    left_proj = lax.psum(dot_t(act_rows, flat_piece), "tensor")
    valid_rows = (lax.broadcasted_iota(jnp.int32, (seq_len, 1), 0) < lengths[0]).astype(jnp.float32)
    products = jnp.sum(left_proj * right_proj * valid_rows, axis=0).reshape(rank_count, query_count)
    partial_scores = (jnp.sum(products, axis=0) / math.sqrt(seq_len * rank_count)).reshape(
        1, query_count
    )
    return lax.psum(partial_scores, "tensor")


def solution(mesh):
    line = mesh.shape["dp"] == 4 and mesh.shape["tensor"] == 4
    return jax.shard_map(
        line_shards if line else gather_shards,
        mesh=mesh,
        in_specs=(
            P("dp", "groups", "tensor"),
            P("dp", "groups", "tensor"),
            P(("groups", "dp")),
            P(None, "groups", "dp"),
            P("dp", "groups", "tensor"),
        ),
        out_specs=P("dp", "groups"),
        check_vma=False,
    )
```

```python
import math

import jax
import jax.numpy as jnp
from jax import lax
from jax.sharding import PartitionSpec as P

RANK = 32

EDGE = [(0, 1), (1, 0), (2, 3), (3, 2)]
INWARD = [(0, 1), (3, 2)]
OUTWARD = [(1, 0), (2, 3)]
MIDDLE = [(1, 2), (2, 1)]


def after(value, *earlier):
    return lax.optimization_barrier((value, *earlier))[0]


def dot_t(a, b):
    return lax.dot_general(a, b, (((1,), (1,)), ((), ())), preferred_element_type=jnp.float32)


def line_shards(activations, out_grads, lengths, query_left, query_right):
    seq_len = activations.shape[1]
    act = activations.reshape(seq_len, activations.shape[2])
    grad = out_grads.reshape(seq_len, out_grads.shape[2])
    rank_count = RANK
    query_count = query_left.shape[1]
    lanes = lax.axis_size("tensor")
    node = lax.axis_index("dp")
    lane = lax.axis_index("tensor")
    left_rows = query_left.reshape(rank_count * query_count, query_left.shape[2])
    block = query_right.shape[0] * query_count
    right_rows = query_right.reshape(block, query_right.shape[2])
    width = right_rows.shape[1]
    piece = width // 7
    cut1, cut2 = 2 * piece, 4 * piece
    share = left_rows.shape[1] // lanes

    def hop(value, pairs):
        return lax.ppermute(value, "dp", pairs)

    def swap(value, distance):
        return lax.ppermute(value, "tensor", [(k, k ^ distance) for k in range(lanes)])

    def part(value, index):
        return lax.dynamic_slice_in_dim(value, index * share, share, 1)

    left_own = part(left_rows, lane)
    y1_own = right_rows[:, :cut1]
    y2_own = right_rows[:, cut1:cut2]
    x_own = right_rows[:, cut2:]

    left_edge = hop(left_own, EDGE)
    left_mid = hop(left_own, MIDDLE)
    y1_edge = hop(y1_own, EDGE)
    y1_mid = hop(y1_own, MIDDLE)
    left_far = hop(left_edge, MIDDLE)
    left_out = hop(left_mid, OUTWARD)
    y2_own_b = after(y2_own, left_edge, left_mid)
    y2_edge = hop(y2_own_b, EDGE)
    y2_mid = hop(after(y2_own_b, y1_mid), MIDDLE)
    x_own_b = after(x_own, y1_edge)
    x_edge = hop(x_own_b, INWARD)
    left_outfar = hop(left_far, OUTWARD)
    x_mid = hop(after(x_own_b, left_far), MIDDLE)
    y1_out = hop(after(y1_mid, y2_edge), OUTWARD)
    grad_x = grad[:, cut2:]
    grad_edge = hop(after(grad_x, y2_edge), INWARD)
    y1_far = hop(after(y1_edge, y2_mid), MIDDLE)
    y2_out = hop(after(y2_mid, left_outfar), OUTWARD)
    y2_far = hop(after(y2_edge, x_mid), MIDDLE)
    y1_outfar = hop(after(y1_far, y1_out), OUTWARD)
    x_far = hop(after(x_edge, y1_far), MIDDLE)
    y2_outfar = hop(after(y2_far, y2_out), OUTWARD)

    acts = jnp.stack([act[:, k * share : (k + 1) * share] for k in range(lanes)])
    acts = lax.all_to_all(acts, "tensor", 0, 0, tiled=True)
    third = jnp.where(node < 2, 2, 1)
    fourth = jnp.where(node < 2, 3, 0)
    order = (node, node ^ 1, third, fourth)
    lefts = (left_own, left_edge, left_mid + left_out, left_far + left_outfar)
    left = 0.0
    for position, rows in zip(order, lefts):
        mine = lax.dynamic_index_in_dim(acts, position, 0, keepdims=False)
        left = left + dot_t(mine, rows)
    distance = 1
    while distance < lanes:
        left = left + swap(left, distance)
        distance *= 2
    valid_rows = (lax.broadcasted_iota(jnp.int32, (seq_len, 1), 0) < lengths[0]).astype(jnp.float32)
    left = left * valid_rows
    left_end = hop(after(left, grad_edge), INWARD)

    is_mid = jnp.logical_or(node == 1, node == 2).astype(jnp.float32)
    left_both = jnp.concatenate([left * is_mid, left_end], axis=0)
    grad_both = jnp.concatenate([grad_x, grad_edge], axis=0)
    y1s = (y1_own, y1_edge, y1_mid + y1_out, y1_far + y1_outfar)
    y2s = (y2_own, y2_edge, y2_mid + y2_out, y2_far + y2_outfar)
    xs = (x_own, x_edge, x_mid, x_far)
    own = jnp.zeros((block,), jnp.float32)
    end = jnp.zeros((block,), jnp.float32)
    for position, y1, y2, x in zip(order, y1s, y2s, xs):
        right_y = dot_t(grad[:, :cut1], y1) + dot_t(grad[:, cut1:cut2], y2)
        right_x = dot_t(grad_both, x)
        columns = lax.dynamic_slice_in_dim(left, position * block, block, 1)
        columns_both = lax.dynamic_slice_in_dim(left_both, position * block, block, 1)
        own = own + jnp.sum(columns * right_y, axis=0)
        product = columns_both * right_x
        own = own + jnp.sum(product[:seq_len], axis=0)
        end = end + jnp.sum(product[seq_len:], axis=0)

    def per_query(value):
        return jnp.sum(value.reshape(block // query_count, query_count), axis=0)[None]

    end = hop(per_query(end), OUTWARD)
    total = (per_query(own) + end) / math.sqrt(seq_len * rank_count)
    distance = 1
    while distance < lanes:
        total = total + swap(total, distance)
        distance *= 2
    return total


def gather_shards(activations, out_grads, lengths, query_left, query_right):
    seq_len = activations.shape[1]
    act_rows = activations.reshape(seq_len, activations.shape[2])
    grad_rows = out_grads.reshape(seq_len, out_grads.shape[2])
    rank_count = RANK
    query_count = query_left.shape[1]
    shard_piece = lax.all_gather(query_right, "dp", axis=0, tiled=True)
    flat_piece = shard_piece.reshape(shard_piece.shape[0] * query_count, shard_piece.shape[2])
    right_proj = dot_t(grad_rows, flat_piece)
    rank_blocks = lax.all_to_all(query_left, "dp", split_axis=0, concat_axis=2, tiled=True)
    slice_width = act_rows.shape[1]
    offset = lax.axis_index("tensor") * slice_width
    own_columns = lax.dynamic_slice_in_dim(rank_blocks, offset, slice_width, 2)
    shard_piece = lax.all_gather(own_columns, "dp", axis=0, tiled=True)
    flat_piece = shard_piece.reshape(shard_piece.shape[0] * query_count, slice_width)
    left_proj = lax.psum(dot_t(act_rows, flat_piece), "tensor")
    valid_rows = (lax.broadcasted_iota(jnp.int32, (seq_len, 1), 0) < lengths[0]).astype(jnp.float32)
    products = jnp.sum(left_proj * right_proj * valid_rows, axis=0).reshape(rank_count, query_count)
    partial_scores = (jnp.sum(products, axis=0) / math.sqrt(seq_len * rank_count)).reshape(
        1, query_count
    )
    return lax.psum(partial_scores, "tensor")


def solution(mesh):
    line = mesh.shape["dp"] == 4 and mesh.shape["tensor"] == 4
    return jax.shard_map(
        line_shards if line else gather_shards,
        mesh=mesh,
        in_specs=(
            P("dp", "groups", "tensor"),
            P("dp", "groups", "tensor"),
            P(("groups", "dp")),
            P(None, "groups", "dp"),
            P("dp", "groups", "tensor"),
        ),
        out_specs=P("dp", "groups"),
        check_vma=False,
    )
```

```python
import math

import jax
import jax.numpy as jnp
from jax import lax
from jax.sharding import PartitionSpec as P

RANK = 32

EDGE = [(0, 1), (1, 0), (2, 3), (3, 2)]
INWARD = [(0, 1), (3, 2)]
OUTWARD = [(1, 0), (2, 3)]
MIDDLE = [(1, 2), (2, 1)]

WAITS = {
    "mmX": ("exY", "a2a", "exL"),
    "inG": ("exY", "mmL", "a2a"),
    "mmY1e": ("inX", "outLf"),
    "mmY2e": ("mmX",),
    "mmXe": ("mmY1e", "x"),
    "outY2f": ("outYm", "x"),
    "inLeft": ("mmY2e", "mmY1e", "outYm"),
    "outLm": ("exL", "mmL"),
    "outLf": ("outLm", "mmY", "exY"),
    "x": ("inX", "mmLe"),
    "outYm": ("outLm", "a2a"),
    "outY1f": ("inX",),
    "inX": ("exL",),
    "a2a": ("exL",),
}


def after(value, *earlier):
    return lax.optimization_barrier((value, *earlier))[0]


def dot_t(a, b):
    return lax.dot_general(a, b, (((1,), (1,)), ((), ())), preferred_element_type=jnp.float32)


def line_shards(activations, out_grads, lengths, query_left, query_right):
    seq_len = activations.shape[1]
    act = activations.reshape(seq_len, activations.shape[2])
    grad = out_grads.reshape(seq_len, out_grads.shape[2])
    rank_count = RANK
    query_count = query_left.shape[1]
    lanes = lax.axis_size("tensor")
    node = lax.axis_index("dp")
    lane = lax.axis_index("tensor")
    left_rows = query_left.reshape(rank_count * query_count, query_left.shape[2])
    block = query_right.shape[0] * query_count
    right_rows = query_right.reshape(block, query_right.shape[2])
    width = right_rows.shape[1]
    piece = width // 7
    cut1, cut2 = 2 * piece, 4 * piece
    share = left_rows.shape[1] // lanes
    got = {}

    def wait(name, value):
        earlier = [got[other] for other in WAITS.get(name, ())]
        return after(value, *earlier) if earlier else value

    def hop(name, value, pairs):
        got[name] = lax.ppermute(wait(name, value), "dp", pairs)
        return got[name]

    def swap(name, value, distance):
        got[name] = lax.ppermute(
            wait(name, value), "tensor", [(k, k ^ distance) for k in range(lanes)]
        )
        return got[name]

    left_own = lax.dynamic_slice_in_dim(left_rows, lane * share, share, 1)
    y_own = right_rows[:, :cut2]
    x_own = right_rows[:, cut2:]
    grad_x = grad[:, cut2:]

    left_edge = hop("exL", left_own, EDGE)
    left_mid = hop("mmL", left_own, MIDDLE)
    y_edge = hop("exY", y_own, EDGE)
    y_mid = hop("mmY", y_own, MIDDLE)
    acts = jnp.stack([act[:, k * share : (k + 1) * share] for k in range(lanes)])
    acts = lax.all_to_all(wait("a2a", acts), "tensor", 0, 0, tiled=True)
    got["a2a"] = acts
    left_far = hop("mmLe", left_edge, MIDDLE)
    left_out = hop("outLm", left_mid, OUTWARD)
    x_edge = hop("inX", x_own, INWARD)
    x_mid = hop("mmX", x_own, MIDDLE)
    left_outfar = hop("outLf", left_far, OUTWARD)
    grad_edge = hop("inG", grad_x, INWARD)
    y1_far = hop("mmY1e", y_edge[:, :cut1], MIDDLE)
    y_out = hop("outYm", y_mid, OUTWARD)
    third = jnp.where(node < 2, 2, 1)
    fourth = jnp.where(node < 2, 3, 0)
    order = (node, node ^ 1, third, fourth)
    lefts = (left_own, left_edge, left_mid + left_out, left_far + left_outfar)
    left = 0.0
    for position, rows in zip(order, lefts):
        own_act = lax.dynamic_index_in_dim(acts, position, 0, keepdims=False)
        left = left + dot_t(own_act, rows)
    left = left + swap("core", left, 1)
    left = left + swap("x", left, 2)
    valid_rows = (lax.broadcasted_iota(jnp.int32, (seq_len, 1), 0) < lengths[0]).astype(jnp.float32)
    left = left * valid_rows

    y2_far = hop("mmY2e", y_edge[:, cut1:], MIDDLE)
    y1_outfar = hop("outY1f", y1_far, OUTWARD)
    x_far = hop("mmXe", x_edge, MIDDLE)
    left_end = hop("inLeft", left, INWARD)
    y2_outfar = hop("outY2f", y2_far, OUTWARD)

    is_mid = jnp.logical_or(node == 1, node == 2).astype(jnp.float32)
    left_both = jnp.concatenate([left * is_mid, left_end], axis=0)
    grad_both = jnp.concatenate([grad_x, grad_edge], axis=0)
    ys = (y_own, y_edge, y_mid + y_out)
    xs = (x_own, x_edge, x_mid, x_far)
    early_x = lax.optimization_barrier([dot_t(grad_both, x) for x in xs[:3]])
    early_y = lax.optimization_barrier(
        [dot_t(grad[:, :cut2], y) for y in ys]
    )
    right_x = early_x + [dot_t(grad_both, xs[3])]
    y1, y2 = y1_far + y1_outfar, y2_far + y2_outfar
    right_y = early_y + [dot_t(grad[:, :cut1], y1) + dot_t(grad[:, cut1:cut2], y2)]
    own = jnp.zeros((block,), jnp.float32)
    end = jnp.zeros((block,), jnp.float32)
    for position, x, y in zip(order, right_x, right_y):
        columns = lax.dynamic_slice_in_dim(left, position * block, block, 1)
        columns_both = lax.dynamic_slice_in_dim(left_both, position * block, block, 1)
        own = own + jnp.sum(columns * y, axis=0)
        product = columns_both * x
        own = own + jnp.sum(product[:seq_len], axis=0)
        end = end + jnp.sum(product[seq_len:], axis=0)

    def per_query(value):
        return jnp.sum(value.reshape(block // query_count, query_count), axis=0)[None]

    end = hop("end", per_query(end), OUTWARD)
    total = (per_query(own) + end) / math.sqrt(seq_len * rank_count)
    total = total + swap("sum1", total, 1)
    total = total + swap("sum2", total, 2)
    return total


def gather_shards(activations, out_grads, lengths, query_left, query_right):
    seq_len = activations.shape[1]
    act_rows = activations.reshape(seq_len, activations.shape[2])
    grad_rows = out_grads.reshape(seq_len, out_grads.shape[2])
    rank_count = RANK
    query_count = query_left.shape[1]
    shard_piece = lax.all_gather(query_right, "dp", axis=0, tiled=True)
    flat_piece = shard_piece.reshape(shard_piece.shape[0] * query_count, shard_piece.shape[2])
    right_proj = dot_t(grad_rows, flat_piece)
    rank_blocks = lax.all_to_all(query_left, "dp", split_axis=0, concat_axis=2, tiled=True)
    slice_width = act_rows.shape[1]
    offset = lax.axis_index("tensor") * slice_width
    own_columns = lax.dynamic_slice_in_dim(rank_blocks, offset, slice_width, 2)
    shard_piece = lax.all_gather(own_columns, "dp", axis=0, tiled=True)
    flat_piece = shard_piece.reshape(shard_piece.shape[0] * query_count, slice_width)
    left_proj = lax.psum(dot_t(act_rows, flat_piece), "tensor")
    valid_rows = (lax.broadcasted_iota(jnp.int32, (seq_len, 1), 0) < lengths[0]).astype(jnp.float32)
    products = jnp.sum(left_proj * right_proj * valid_rows, axis=0).reshape(rank_count, query_count)
    partial_scores = (jnp.sum(products, axis=0) / math.sqrt(seq_len * rank_count)).reshape(
        1, query_count
    )
    return lax.psum(partial_scores, "tensor")


def solution(mesh):
    line = mesh.shape["dp"] == 4 and mesh.shape["tensor"] == 4
    return jax.shard_map(
        line_shards if line else gather_shards,
        mesh=mesh,
        in_specs=(
            P("dp", "groups", "tensor"),
            P("dp", "groups", "tensor"),
            P(("groups", "dp")),
            P(None, "groups", "dp"),
            P("dp", "groups", "tensor"),
        ),
        out_specs=P("dp", "groups"),
        check_vma=False,
    )
```

```python
import math

import jax
import jax.numpy as jnp
from jax import lax
from jax.sharding import PartitionSpec as P

RANK = 32

EDGE = [(0, 1), (1, 0), (2, 3), (3, 2)]
INWARD = [(0, 1), (3, 2)]
OUTWARD = [(1, 0), (2, 3)]
MIDDLE = [(1, 2), (2, 1)]

SCHEDULE = [
    ("mmY", ()),
    ("exL", ()),
    ("exY", ()),
    ("mmL", ()),
    ("inX", ("exL", "act")),
    ("outLm", ("mmL",)),
    ("mmX", ("exY", "exL", "mmL")),
    ("a2a", ("exL", "mmL")),
    ("mmLe", ()),
    ("outLf", ("mmY", "exY")),
    ("core", ("a2a", "exY")),
    ("outYm", ("outLm", "a2a")),
    ("lanes", ("inX",)),
    ("mmY1e", ("inX", "outLf")),
    ("inLeft", ("outYm", "core", "a2a")),
    ("inG", ("exY", "a2a", "mmLe")),
    ("outY1f", ("mmX", "outLf")),
    ("mmY2e", ("mmX", "mmLe", "outLf")),
    ("mmXe", ("mmY1e", "core")),
    ("outY2f", ("lanes",)),
]
CUT1, CUT2 = 15, 29


def after(value, *earlier):
    return lax.optimization_barrier((value, *earlier))[0]


def swap(value, distance):
    lanes = lax.axis_size("tensor")
    return lax.ppermute(value, "tensor", [(k, k ^ distance) for k in range(lanes)])


def dot_t(a, b):
    return lax.dot_general(a, b, (((1,), (1,)), ((), ())), preferred_element_type=jnp.float32)


def line_shards(activations, out_grads, lengths, query_left, query_right):
    seq_len = activations.shape[1]
    act = activations.reshape(seq_len, activations.shape[2])
    grad = out_grads.reshape(seq_len, out_grads.shape[2])
    rank_count = RANK
    query_count = query_left.shape[1]
    lanes = lax.axis_size("tensor")
    node = lax.axis_index("dp")
    lane = lax.axis_index("tensor")
    left_rows = query_left.reshape(rank_count * query_count, query_left.shape[2])
    block = query_right.shape[0] * query_count
    right_rows = query_right.reshape(block, query_right.shape[2])
    unit = right_rows.shape[1] // 56
    cut1, cut2 = CUT1 * unit, CUT2 * unit
    share = left_rows.shape[1] // lanes
    third = jnp.where(node < 2, 2, 1)
    fourth = jnp.where(node < 2, 3, 0)
    order = (node, node ^ 1, third, fourth)

    got = {
        "left": lax.dynamic_slice_in_dim(left_rows, lane * share, share, 1),
        "y": right_rows[:, :cut2],
        "x": right_rows[:, cut2:],
        "grad": grad[:, cut2:],
        "act": jnp.stack([act[:, k * share : (k + 1) * share] for k in range(lanes)]),
    }

    def left_partial():
        lefts = (
            got["left"],
            got["exL"],
            got["mmL"] + got["outLm"],
            got["mmLe"] + got["outLf"],
        )
        total = 0.0
        for position, rows in zip(order, lefts):
            own_act = lax.dynamic_index_in_dim(got["a2a"], position, 0, keepdims=False)
            total = total + dot_t(own_act, rows)
        got["partial"] = total
        return total

    def left_pair():
        got["pair"] = got["partial"] + got["core"]
        return got["pair"]

    def left_masked():
        rows = lax.broadcasted_iota(jnp.int32, (seq_len, 1), 0)
        valid = (rows < lengths[0]).astype(jnp.float32)
        got["masked"] = (got["pair"] + got["lanes"]) * valid
        return got["masked"]

    operands = {
        "exL": (lambda: got["left"], EDGE),
        "mmL": (lambda: got["left"], MIDDLE),
        "exY": (lambda: got["y"], EDGE),
        "mmY": (lambda: got["y"], MIDDLE),
        "a2a": (lambda: got["act"], None),
        "mmLe": (lambda: got["exL"], MIDDLE),
        "outLm": (lambda: got["mmL"], OUTWARD),
        "inX": (lambda: got["x"], INWARD),
        "mmX": (lambda: got["x"], MIDDLE),
        "outLf": (lambda: got["mmLe"], OUTWARD),
        "inG": (lambda: got["grad"], INWARD),
        "mmY1e": (lambda: got["exY"][:, :cut1], MIDDLE),
        "outYm": (lambda: got["mmY"], OUTWARD),
        "core": (left_partial, 1),
        "lanes": (left_pair, 2),
        "mmY2e": (lambda: got["exY"][:, cut1:], MIDDLE),
        "outY1f": (lambda: got["mmY1e"], OUTWARD),
        "mmXe": (lambda: got["inX"], MIDDLE),
        "inLeft": (left_masked, INWARD),
        "outY2f": (lambda: got["mmY2e"], OUTWARD),
    }
    for name, waits in SCHEDULE:
        make, route = operands[name]
        value = make()
        if waits:
            value = after(value, *[got[other] for other in waits])
        if route is None:
            got[name] = lax.all_to_all(value, "tensor", 0, 0, tiled=True)
        elif isinstance(route, int):
            got[name] = swap(value, route)
        else:
            got[name] = lax.ppermute(value, "dp", route)

    left, left_end = got["masked"], got["inLeft"]
    is_mid = jnp.logical_or(node == 1, node == 2).astype(jnp.float32)
    left_both = jnp.concatenate([left * is_mid, left_end], axis=0)
    grad_both = jnp.concatenate([got["grad"], got["inG"]], axis=0)
    xs = (got["x"], got["inX"], got["mmX"])
    ys = (got["y"], got["exY"], got["mmY"] + got["outYm"])
    early_x = lax.optimization_barrier([dot_t(grad_both, x) for x in xs])
    early_y = lax.optimization_barrier([dot_t(grad[:, :cut2], y) for y in ys])
    early_last = dot_t(grad[:, :cut1], got["mmY1e"] + got["outY1f"])
    early_last = lax.optimization_barrier(early_last)
    grad_last = grad[:, cut1:cut2]
    right_x = early_x + [dot_t(grad_both, got["mmXe"])]
    own = jnp.zeros((block,), jnp.float32)
    end = jnp.zeros((block,), jnp.float32)
    for position, x in zip(order, right_x):
        product = lax.dynamic_slice_in_dim(left_both, position * block, block, 1) * x
        own = own + jnp.sum(product[:seq_len], axis=0)
        end = end + jnp.sum(product[seq_len:], axis=0)

    def per_query(value):
        return jnp.sum(value.reshape(block // query_count, query_count), axis=0)[None]

    end = per_query(end)
    grad_last = after(grad_last, end)
    end = lax.ppermute(end, "dp", OUTWARD)
    y2 = got["mmY2e"] + got["outY2f"]
    right_y = early_y + [early_last + dot_t(grad_last, y2)]
    for position, y in zip(order, right_y):
        own = own + jnp.sum(lax.dynamic_slice_in_dim(left, position * block, block, 1) * y, axis=0)
    total = (per_query(own) + end) / math.sqrt(seq_len * rank_count)
    total = total + swap(total, 1)
    total = total + swap(total, 2)
    return total


def gather_shards(activations, out_grads, lengths, query_left, query_right):
    seq_len = activations.shape[1]
    act_rows = activations.reshape(seq_len, activations.shape[2])
    grad_rows = out_grads.reshape(seq_len, out_grads.shape[2])
    rank_count = RANK
    query_count = query_left.shape[1]
    shard_piece = lax.all_gather(query_right, "dp", axis=0, tiled=True)
    flat_piece = shard_piece.reshape(shard_piece.shape[0] * query_count, shard_piece.shape[2])
    right_proj = dot_t(grad_rows, flat_piece)
    rank_blocks = lax.all_to_all(query_left, "dp", split_axis=0, concat_axis=2, tiled=True)
    slice_width = act_rows.shape[1]
    offset = lax.axis_index("tensor") * slice_width
    own_columns = lax.dynamic_slice_in_dim(rank_blocks, offset, slice_width, 2)
    shard_piece = lax.all_gather(own_columns, "dp", axis=0, tiled=True)
    flat_piece = shard_piece.reshape(shard_piece.shape[0] * query_count, slice_width)
    left_proj = lax.psum(dot_t(act_rows, flat_piece), "tensor")
    valid_rows = (lax.broadcasted_iota(jnp.int32, (seq_len, 1), 0) < lengths[0]).astype(jnp.float32)
    products = jnp.sum(left_proj * right_proj * valid_rows, axis=0).reshape(rank_count, query_count)
    partial_scores = (jnp.sum(products, axis=0) / math.sqrt(seq_len * rank_count)).reshape(
        1, query_count
    )
    return lax.psum(partial_scores, "tensor")


def solution(mesh):
    line = mesh.shape["dp"] == 4 and mesh.shape["tensor"] == 4
    return jax.shard_map(
        line_shards if line else gather_shards,
        mesh=mesh,
        in_specs=(
            P("dp", "groups", "tensor"),
            P("dp", "groups", "tensor"),
            P(("groups", "dp")),
            P(None, "groups", "dp"),
            P("dp", "groups", "tensor"),
        ),
        out_specs=P("dp", "groups"),
        check_vma=False,
    )
```

```python
import math

import jax
import jax.numpy as jnp
from jax import lax
from jax.sharding import PartitionSpec as P

RANK = 32

EDGE = [(0, 1), (1, 0), (2, 3), (3, 2)]
INWARD = [(0, 1), (3, 2)]
OUTWARD = [(1, 0), (2, 3)]
MIDDLE = [(1, 2), (2, 1)]

SCHEDULE = [
    ("exL", ()),
    ("mmY", ()),
    ("mmL", ()),
    ("inX", ("exL", "act", "mmL")),
    ("exY", ()),
    ("outLm", ("mmL",)),
    ("mmX", ("exY", "exL", "mmL")),
    ("a2a", ("exL", "mmL")),
    ("mmLe", ()),
    ("outLf", ("mmY", "exY")),
    ("core", ("a2a", "exY")),
    ("outYm", ("outLm", "a2a")),
    ("lanes", ("inX", "mmLe", "core")),
    ("mmY1e", ("inX", "outLf")),
    ("inLeft", ("outYm", "core", "a2a")),
    ("outY1f", ("mmX", "outLf")),
    ("inG", ("exY", "a2a")),
    ("mmY2e", ("mmX", "mmLe", "outLf")),
    ("outY2f", ("lanes", "core", "outYm")),
    ("mmXe", ("mmY1e", "core", "outYm")),
]
CUT1, CUT2 = 12, 31


def after(value, *earlier):
    return lax.optimization_barrier((value, *earlier))[0]


def swap(value, distance):
    lanes = lax.axis_size("tensor")
    return lax.ppermute(value, "tensor", [(k, k ^ distance) for k in range(lanes)])


def dot_t(a, b):
    return lax.dot_general(a, b, (((1,), (1,)), ((), ())), preferred_element_type=jnp.float32)


def line_shards(activations, out_grads, lengths, query_left, query_right):
    seq_len = activations.shape[1]
    act = activations.reshape(seq_len, activations.shape[2])
    grad = out_grads.reshape(seq_len, out_grads.shape[2])
    rank_count = RANK
    query_count = query_left.shape[1]
    lanes = lax.axis_size("tensor")
    node = lax.axis_index("dp")
    lane = lax.axis_index("tensor")
    left_rows = query_left.reshape(rank_count * query_count, query_left.shape[2])
    block = query_right.shape[0] * query_count
    right_rows = query_right.reshape(block, query_right.shape[2])
    unit = right_rows.shape[1] // 56
    cut1, cut2 = CUT1 * unit, CUT2 * unit
    share = left_rows.shape[1] // lanes
    third = jnp.where(node < 2, 2, 1)
    fourth = jnp.where(node < 2, 3, 0)
    order = (node, node ^ 1, third, fourth)

    got = {
        "left": lax.dynamic_slice_in_dim(left_rows, lane * share, share, 1),
        "y": right_rows[:, :cut2],
        "x": right_rows[:, cut2:],
        "grad": grad[:, cut2:],
        "act": jnp.stack([act[:, k * share : (k + 1) * share] for k in range(lanes)]),
    }

    def left_partial():
        lefts = (
            got["left"],
            got["exL"],
            got["mmL"] + got["outLm"],
            got["mmLe"] + got["outLf"],
        )
        total = 0.0
        for position, rows in zip(order, lefts):
            own_act = lax.dynamic_index_in_dim(got["a2a"], position, 0, keepdims=False)
            total = total + dot_t(own_act, rows)
        got["partial"] = total
        return total

    def left_pair():
        got["pair"] = got["partial"] + got["core"]
        return got["pair"]

    def left_masked():
        rows = lax.broadcasted_iota(jnp.int32, (seq_len, 1), 0)
        valid = (rows < lengths[0]).astype(jnp.float32)
        got["masked"] = (got["pair"] + got["lanes"]) * valid
        return got["masked"]

    operands = {
        "exL": (lambda: got["left"], EDGE),
        "mmL": (lambda: got["left"], MIDDLE),
        "exY": (lambda: got["y"], EDGE),
        "mmY": (lambda: got["y"], MIDDLE),
        "a2a": (lambda: got["act"], None),
        "mmLe": (lambda: got["exL"], MIDDLE),
        "outLm": (lambda: got["mmL"], OUTWARD),
        "inX": (lambda: got["x"], INWARD),
        "mmX": (lambda: got["x"], MIDDLE),
        "outLf": (lambda: got["mmLe"], OUTWARD),
        "inG": (lambda: got["grad"], INWARD),
        "mmY1e": (lambda: got["exY"][:, :cut1], MIDDLE),
        "outYm": (lambda: got["mmY"], OUTWARD),
        "core": (left_partial, 1),
        "lanes": (left_pair, 2),
        "mmY2e": (lambda: got["exY"][:, cut1:], MIDDLE),
        "outY1f": (lambda: got["mmY1e"], OUTWARD),
        "mmXe": (lambda: got["inX"], MIDDLE),
        "inLeft": (left_masked, INWARD),
        "outY2f": (lambda: got["mmY2e"], OUTWARD),
    }
    for name, waits in SCHEDULE:
        make, route = operands[name]
        value = make()
        if waits:
            value = after(value, *[got[other] for other in waits])
        if route is None:
            got[name] = lax.all_to_all(value, "tensor", 0, 0, tiled=True)
        elif isinstance(route, int):
            got[name] = swap(value, route)
        else:
            got[name] = lax.ppermute(value, "dp", route)

    left, left_end = got["masked"], got["inLeft"]
    is_mid = jnp.logical_or(node == 1, node == 2).astype(jnp.float32)
    left_both = jnp.concatenate([left * is_mid, left_end], axis=0)
    grad_both = jnp.concatenate([got["grad"], got["inG"]], axis=0)
    xs = (got["x"], got["inX"], got["mmX"])
    ys = (got["y"], got["exY"], got["mmY"] + got["outYm"])
    early_x = lax.optimization_barrier([dot_t(grad_both, x) for x in xs])
    early_y = lax.optimization_barrier([dot_t(grad[:, :cut2], y) for y in ys])
    early_last = dot_t(grad[:, :cut1], got["mmY1e"] + got["outY1f"])
    early_last = lax.optimization_barrier(early_last)
    grad_last = grad[:, cut1:cut2]
    right_x = early_x + [dot_t(grad_both, got["mmXe"])]
    own = jnp.zeros((block,), jnp.float32)
    end = jnp.zeros((block,), jnp.float32)
    for position, x in zip(order, right_x):
        product = lax.dynamic_slice_in_dim(left_both, position * block, block, 1) * x
        own = own + jnp.sum(product[:seq_len], axis=0)
        end = end + jnp.sum(product[seq_len:], axis=0)

    def per_query(value):
        return jnp.sum(value.reshape(block // query_count, query_count), axis=0)[None]

    end = per_query(end)
    grad_last = after(grad_last, end)
    end = lax.ppermute(end, "dp", OUTWARD)
    y2 = got["mmY2e"] + got["outY2f"]
    right_y = early_y + [early_last + dot_t(grad_last, y2)]
    for position, y in zip(order, right_y):
        own = own + jnp.sum(lax.dynamic_slice_in_dim(left, position * block, block, 1) * y, axis=0)
    total = (per_query(own) + end) / math.sqrt(seq_len * rank_count)
    total = total + swap(total, 1)
    total = total + swap(total, 2)
    return total


def gather_shards(activations, out_grads, lengths, query_left, query_right):
    seq_len = activations.shape[1]
    act_rows = activations.reshape(seq_len, activations.shape[2])
    grad_rows = out_grads.reshape(seq_len, out_grads.shape[2])
    rank_count = RANK
    query_count = query_left.shape[1]
    shard_piece = lax.all_gather(query_right, "dp", axis=0, tiled=True)
    flat_piece = shard_piece.reshape(shard_piece.shape[0] * query_count, shard_piece.shape[2])
    right_proj = dot_t(grad_rows, flat_piece)
    rank_blocks = lax.all_to_all(query_left, "dp", split_axis=0, concat_axis=2, tiled=True)
    slice_width = act_rows.shape[1]
    offset = lax.axis_index("tensor") * slice_width
    own_columns = lax.dynamic_slice_in_dim(rank_blocks, offset, slice_width, 2)
    shard_piece = lax.all_gather(own_columns, "dp", axis=0, tiled=True)
    flat_piece = shard_piece.reshape(shard_piece.shape[0] * query_count, slice_width)
    left_proj = lax.psum(dot_t(act_rows, flat_piece), "tensor")
    valid_rows = (lax.broadcasted_iota(jnp.int32, (seq_len, 1), 0) < lengths[0]).astype(jnp.float32)
    products = jnp.sum(left_proj * right_proj * valid_rows, axis=0).reshape(rank_count, query_count)
    partial_scores = (jnp.sum(products, axis=0) / math.sqrt(seq_len * rank_count)).reshape(
        1, query_count
    )
    return lax.psum(partial_scores, "tensor")


def solution(mesh):
    line = mesh.shape["dp"] == 4 and mesh.shape["tensor"] == 4
    return jax.shard_map(
        line_shards if line else gather_shards,
        mesh=mesh,
        in_specs=(
            P("dp", "groups", "tensor"),
            P("dp", "groups", "tensor"),
            P(("groups", "dp")),
            P(None, "groups", "dp"),
            P("dp", "groups", "tensor"),
        ),
        out_specs=P("dp", "groups"),
        check_vma=False,
    )
```

```python
import math

import jax
import jax.numpy as jnp
from jax import lax
from jax.sharding import PartitionSpec as P

RANK = 32

EDGE = [(0, 1), (1, 0), (2, 3), (3, 2)]
INWARD = [(0, 1), (3, 2)]
OUTWARD = [(1, 0), (2, 3)]
MIDDLE = [(1, 2), (2, 1)]

SCHEDULE = [
    ("exL", ()),
    ("exY", ()),
    ("mmL", ()),
    ("a2a", ("exL", "act")),
    ("mmY", ()),
    ("inX", ("act", "exL")),
    ("mmLe", ()),
    ("outLf", ("mmY", "mmL")),
    ("outLm", ("exL", "x")),
    ("outYm", ("outLm", "a2a")),
    ("mmX", ("exY", "exL")),
    ("mmY1e", ("inX", "mmLe", "x")),
    ("core", ("exY", "inX", "a2a")),
    ("lanes", ("inX", "outLm", "mmY1e")),
    ("inLeft", ("outYm", "a2a", "outLf")),
    ("inG", ("exY", "a2a", "mmLe")),
    ("outY1f", ("outYm", "core", "outLm")),
    ("mmY2e", ("mmX", "outLf", "outLm")),
    ("outY2f", ("mmY2e", "mmLe", "core")),
    ("mmXe", ("core", "mmY1e")),
]
CUT1, CUT2 = 13, 31


def after(value, *earlier):
    return lax.optimization_barrier((value, *earlier))[0]


def swap(value, distance):
    lanes = lax.axis_size("tensor")
    return lax.ppermute(value, "tensor", [(k, k ^ distance) for k in range(lanes)])


def dot_t(a, b):
    return lax.dot_general(a, b, (((1,), (1,)), ((), ())), preferred_element_type=jnp.float32)


def line_shards(activations, out_grads, lengths, query_left, query_right):
    seq_len = activations.shape[1]
    act = activations.reshape(seq_len, activations.shape[2])
    grad = out_grads.reshape(seq_len, out_grads.shape[2])
    rank_count = RANK
    query_count = query_left.shape[1]
    lanes = lax.axis_size("tensor")
    node = lax.axis_index("dp")
    lane = lax.axis_index("tensor")
    left_rows = query_left.reshape(rank_count * query_count, query_left.shape[2])
    block = query_right.shape[0] * query_count
    right_rows = query_right.reshape(block, query_right.shape[2])
    unit = right_rows.shape[1] // 56
    cut1, cut2 = CUT1 * unit, CUT2 * unit
    share = left_rows.shape[1] // lanes
    third = jnp.where(node < 2, 2, 1)
    fourth = jnp.where(node < 2, 3, 0)
    order = (node, node ^ 1, third, fourth)

    got = {
        "left": lax.dynamic_slice_in_dim(left_rows, lane * share, share, 1),
        "y": right_rows[:, :cut2],
        "x": right_rows[:, cut2:],
        "grad": grad[:, cut2:],
        "act": jnp.stack([act[:, k * share : (k + 1) * share] for k in range(lanes)]),
    }

    def left_partial():
        lefts = (
            got["left"],
            got["exL"],
            got["mmL"] + got["outLm"],
            got["mmLe"] + got["outLf"],
        )
        total = 0.0
        for position, rows in zip(order, lefts):
            own_act = lax.dynamic_index_in_dim(got["a2a"], position, 0, keepdims=False)
            total = total + dot_t(own_act, rows)
        got["partial"] = total
        return total

    def left_pair():
        got["pair"] = got["partial"] + got["core"]
        return got["pair"]

    def left_masked():
        rows = lax.broadcasted_iota(jnp.int32, (seq_len, 1), 0)
        valid = (rows < lengths[0]).astype(jnp.float32)
        got["masked"] = (got["pair"] + got["lanes"]) * valid
        return got["masked"]

    operands = {
        "exL": (lambda: got["left"], EDGE),
        "mmL": (lambda: got["left"], MIDDLE),
        "exY": (lambda: got["y"], EDGE),
        "mmY": (lambda: got["y"], MIDDLE),
        "a2a": (lambda: got["act"], None),
        "mmLe": (lambda: got["exL"], MIDDLE),
        "outLm": (lambda: got["mmL"], OUTWARD),
        "inX": (lambda: got["x"], INWARD),
        "mmX": (lambda: got["x"], MIDDLE),
        "outLf": (lambda: got["mmLe"], OUTWARD),
        "inG": (lambda: got["grad"], INWARD),
        "mmY1e": (lambda: got["exY"][:, :cut1], MIDDLE),
        "outYm": (lambda: got["mmY"], OUTWARD),
        "core": (left_partial, 1),
        "lanes": (left_pair, 2),
        "mmY2e": (lambda: got["exY"][:, cut1:], MIDDLE),
        "outY1f": (lambda: got["mmY1e"], OUTWARD),
        "mmXe": (lambda: got["inX"], MIDDLE),
        "inLeft": (left_masked, INWARD),
        "outY2f": (lambda: got["mmY2e"], OUTWARD),
    }
    for name, waits in SCHEDULE:
        make, route = operands[name]
        value = make()
        if waits:
            value = after(value, *[got[other] for other in waits])
        if route is None:
            got[name] = lax.all_to_all(value, "tensor", 0, 0, tiled=True)
        elif isinstance(route, int):
            got[name] = swap(value, route)
        else:
            got[name] = lax.ppermute(value, "dp", route)

    left, left_end = got["masked"], got["inLeft"]
    is_mid = jnp.logical_or(node == 1, node == 2).astype(jnp.float32)
    columns = [lax.dynamic_slice_in_dim(left, p * block, block, 1) for p in order]
    columns_end = [lax.dynamic_slice_in_dim(left_end, p * block, block, 1) for p in order]
    xs = (got["x"], got["inX"], got["mmX"])
    ys = (got["y"], got["exY"], got["mmY"] + got["outYm"])
    early = [
        dot_t(grad[:, :cut2], y) + is_mid * dot_t(got["grad"], x) for x, y in zip(xs, ys)
    ]
    early.append(dot_t(grad[:, :cut1], got["mmY1e"] + got["outY1f"]))
    early = lax.optimization_barrier(early)
    early_end = lax.optimization_barrier([dot_t(got["inG"], x) for x in xs])
    right_end = early_end + [dot_t(got["inG"], got["mmXe"])]
    end = sum(jnp.sum(c * x, axis=0) for c, x in zip(columns_end, right_end))

    def per_query(value):
        return jnp.sum(value.reshape(block // query_count, query_count), axis=0)[None]

    end = per_query(end)
    grad_own, grad_last = after((got["grad"], grad[:, cut1:cut2]), end)
    end = lax.ppermute(end, "dp", OUTWARD)
    early[3] = early[3] + dot_t(grad_last, got["mmY2e"] + got["outY2f"])
    early[3] = early[3] + is_mid * dot_t(grad_own, got["mmXe"])
    own = sum(jnp.sum(c * y, axis=0) for c, y in zip(columns, early))
    total = (per_query(own) + end) / math.sqrt(seq_len * rank_count)
    total = total + swap(total, 1)
    total = total + swap(total, 2)
    return total


def gather_shards(activations, out_grads, lengths, query_left, query_right):
    seq_len = activations.shape[1]
    act_rows = activations.reshape(seq_len, activations.shape[2])
    grad_rows = out_grads.reshape(seq_len, out_grads.shape[2])
    rank_count = RANK
    query_count = query_left.shape[1]
    shard_piece = lax.all_gather(query_right, "dp", axis=0, tiled=True)
    flat_piece = shard_piece.reshape(shard_piece.shape[0] * query_count, shard_piece.shape[2])
    right_proj = dot_t(grad_rows, flat_piece)
    rank_blocks = lax.all_to_all(query_left, "dp", split_axis=0, concat_axis=2, tiled=True)
    slice_width = act_rows.shape[1]
    offset = lax.axis_index("tensor") * slice_width
    own_columns = lax.dynamic_slice_in_dim(rank_blocks, offset, slice_width, 2)
    shard_piece = lax.all_gather(own_columns, "dp", axis=0, tiled=True)
    flat_piece = shard_piece.reshape(shard_piece.shape[0] * query_count, slice_width)
    left_proj = lax.psum(dot_t(act_rows, flat_piece), "tensor")
    valid_rows = (lax.broadcasted_iota(jnp.int32, (seq_len, 1), 0) < lengths[0]).astype(jnp.float32)
    products = jnp.sum(left_proj * right_proj * valid_rows, axis=0).reshape(rank_count, query_count)
    partial_scores = (jnp.sum(products, axis=0) / math.sqrt(seq_len * rank_count)).reshape(
        1, query_count
    )
    return lax.psum(partial_scores, "tensor")


def solution(mesh):
    line = mesh.shape["dp"] == 4 and mesh.shape["tensor"] == 4
    return jax.shard_map(
        line_shards if line else gather_shards,
        mesh=mesh,
        in_specs=(
            P("dp", "groups", "tensor"),
            P("dp", "groups", "tensor"),
            P(("groups", "dp")),
            P(None, "groups", "dp"),
            P("dp", "groups", "tensor"),
        ),
        out_specs=P("dp", "groups"),
        check_vma=False,
    )
```

```python
import math

import jax
import jax.numpy as jnp
from jax import lax
from jax.sharding import PartitionSpec as P

RANK = 32

EDGE = [(0, 1), (1, 0), (2, 3), (3, 2)]
INWARD = [(0, 1), (3, 2)]
OUTWARD = [(1, 0), (2, 3)]
MIDDLE = [(1, 2), (2, 1)]

SCHEDULE = [
    ("exL", ()),
    ("exY", ("grad",)),
    ("mmL", ()),
    ("a2a", ("act", "mmL")),
    ("mmY", ()),
    ("inX", ("act", "exL")),
    ("mmLe", ()),
    ("outLf", ("mmY", "mmL", "x")),
    ("outLm", ("exL", "x")),
    ("core", ("exY", "inX", "a2a")),
    ("mmX", ("exY", "exL", "mmL")),
    ("outYm", ("outLm", "a2a", "y")),
    ("mmY1e", ("inX", "mmLe", "x")),
    ("lanes", ("outLm", "mmX", "mmY1e")),
    ("outY1f", ("outYm", "core", "outLm")),
    ("inG", ("exY", "a2a", "mmLe")),
    ("inLeft", ("a2a", "outLf", "grad")),
    ("mmY2e", ("mmX", "outLf", "outLm")),
    ("outY2f", ("mmY2e", "mmLe", "core")),
    ("mmXe", ("core", "mmY1e")),
]
CUT1, CUT2 = 12, 31


def after(value, *earlier):
    return lax.optimization_barrier((value, *earlier))[0]


def swap(value, distance):
    lanes = lax.axis_size("tensor")
    return lax.ppermute(value, "tensor", [(k, k ^ distance) for k in range(lanes)])


def dot_t(a, b):
    return lax.dot_general(a, b, (((1,), (1,)), ((), ())), preferred_element_type=jnp.float32)


def line_shards(activations, out_grads, lengths, query_left, query_right):
    seq_len = activations.shape[1]
    act = activations.reshape(seq_len, activations.shape[2])
    grad = out_grads.reshape(seq_len, out_grads.shape[2])
    rank_count = RANK
    query_count = query_left.shape[1]
    lanes = lax.axis_size("tensor")
    node = lax.axis_index("dp")
    lane = lax.axis_index("tensor")
    left_rows = query_left.reshape(rank_count * query_count, query_left.shape[2])
    block = query_right.shape[0] * query_count
    right_rows = query_right.reshape(block, query_right.shape[2])
    unit = right_rows.shape[1] // 56
    cut1, cut2 = CUT1 * unit, CUT2 * unit
    share = left_rows.shape[1] // lanes
    third = jnp.where(node < 2, 2, 1)
    fourth = jnp.where(node < 2, 3, 0)
    order = (node, node ^ 1, third, fourth)

    got = {
        "left": lax.dynamic_slice_in_dim(left_rows, lane * share, share, 1),
        "y": right_rows[:, :cut2],
        "x": right_rows[:, cut2:],
        "grad": grad[:, cut2:],
        "act": jnp.stack([act[:, k * share : (k + 1) * share] for k in range(lanes)]),
    }

    def left_partial():
        lefts = (
            got["left"],
            got["exL"],
            got["mmL"] + got["outLm"],
            got["mmLe"] + got["outLf"],
        )
        total = 0.0
        for position, rows in zip(order, lefts):
            own_act = lax.dynamic_index_in_dim(got["a2a"], position, 0, keepdims=False)
            total = total + dot_t(own_act, rows)
        got["partial"] = total
        return total

    def left_pair():
        got["pair"] = got["partial"] + got["core"]
        return got["pair"]

    def left_masked():
        rows = lax.broadcasted_iota(jnp.int32, (seq_len, 1), 0)
        valid = (rows < lengths[0]).astype(jnp.float32)
        got["masked"] = (got["pair"] + got["lanes"]) * valid
        return got["masked"]

    operands = {
        "exL": (lambda: got["left"], EDGE),
        "mmL": (lambda: got["left"], MIDDLE),
        "exY": (lambda: got["y"], EDGE),
        "mmY": (lambda: got["y"], MIDDLE),
        "a2a": (lambda: got["act"], None),
        "mmLe": (lambda: got["exL"], MIDDLE),
        "outLm": (lambda: got["mmL"], OUTWARD),
        "inX": (lambda: got["x"], INWARD),
        "mmX": (lambda: got["x"], MIDDLE),
        "outLf": (lambda: got["mmLe"], OUTWARD),
        "inG": (lambda: got["grad"], INWARD),
        "mmY1e": (lambda: got["exY"][:, :cut1], MIDDLE),
        "outYm": (lambda: got["mmY"], OUTWARD),
        "core": (left_partial, 1),
        "lanes": (left_pair, 2),
        "mmY2e": (lambda: got["exY"][:, cut1:], MIDDLE),
        "outY1f": (lambda: got["mmY1e"], OUTWARD),
        "mmXe": (lambda: got["inX"], MIDDLE),
        "inLeft": (left_masked, INWARD),
        "outY2f": (lambda: got["mmY2e"], OUTWARD),
    }
    for name, waits in SCHEDULE:
        make, route = operands[name]
        value = make()
        if waits:
            value = after(value, *[got[other] for other in waits])
        if route is None:
            got[name] = lax.all_to_all(value, "tensor", 0, 0, tiled=True)
        elif isinstance(route, int):
            got[name] = swap(value, route)
        else:
            got[name] = lax.ppermute(value, "dp", route)

    left, left_end = got["masked"], got["inLeft"]
    is_mid = jnp.logical_or(node == 1, node == 2).astype(jnp.float32)
    columns = [lax.dynamic_slice_in_dim(left, p * block, block, 1) for p in order]
    columns_end = [lax.dynamic_slice_in_dim(left_end, p * block, block, 1) for p in order]
    xs = (got["x"], got["inX"], got["mmX"])
    ys = (got["y"], got["exY"], got["mmY"] + got["outYm"])
    early = [
        dot_t(grad[:, :cut2], y) + is_mid * dot_t(got["grad"], x) for x, y in zip(xs, ys)
    ]
    early.append(dot_t(grad[:, :cut1], got["mmY1e"] + got["outY1f"]))
    early = lax.optimization_barrier(early)
    early_end = lax.optimization_barrier([dot_t(got["inG"], x) for x in xs])
    right_end = early_end + [dot_t(got["inG"], got["mmXe"])]
    end = sum(jnp.sum(c * x, axis=0) for c, x in zip(columns_end, right_end))

    def per_query(value):
        return jnp.sum(value.reshape(block // query_count, query_count), axis=0)[None]

    end = per_query(end)
    grad_own, grad_last = after((got["grad"], grad[:, cut1:cut2]), end)
    end = lax.ppermute(end, "dp", OUTWARD)
    early[3] = early[3] + dot_t(grad_last, got["mmY2e"] + got["outY2f"])
    early[3] = early[3] + is_mid * dot_t(grad_own, got["mmXe"])
    own = sum(jnp.sum(c * y, axis=0) for c, y in zip(columns, early))
    total = (per_query(own) + end) / math.sqrt(seq_len * rank_count)
    total = total + swap(total, 1)
    total = total + swap(total, 2)
    return total


def gather_shards(activations, out_grads, lengths, query_left, query_right):
    seq_len = activations.shape[1]
    act_rows = activations.reshape(seq_len, activations.shape[2])
    grad_rows = out_grads.reshape(seq_len, out_grads.shape[2])
    rank_count = RANK
    query_count = query_left.shape[1]
    shard_piece = lax.all_gather(query_right, "dp", axis=0, tiled=True)
    flat_piece = shard_piece.reshape(shard_piece.shape[0] * query_count, shard_piece.shape[2])
    right_proj = dot_t(grad_rows, flat_piece)
    rank_blocks = lax.all_to_all(query_left, "dp", split_axis=0, concat_axis=2, tiled=True)
    slice_width = act_rows.shape[1]
    offset = lax.axis_index("tensor") * slice_width
    own_columns = lax.dynamic_slice_in_dim(rank_blocks, offset, slice_width, 2)
    shard_piece = lax.all_gather(own_columns, "dp", axis=0, tiled=True)
    flat_piece = shard_piece.reshape(shard_piece.shape[0] * query_count, slice_width)
    left_proj = lax.psum(dot_t(act_rows, flat_piece), "tensor")
    valid_rows = (lax.broadcasted_iota(jnp.int32, (seq_len, 1), 0) < lengths[0]).astype(jnp.float32)
    products = jnp.sum(left_proj * right_proj * valid_rows, axis=0).reshape(rank_count, query_count)
    partial_scores = (jnp.sum(products, axis=0) / math.sqrt(seq_len * rank_count)).reshape(
        1, query_count
    )
    return lax.psum(partial_scores, "tensor")


def solution(mesh):
    line = mesh.shape["dp"] == 4 and mesh.shape["tensor"] == 4
    return jax.shard_map(
        line_shards if line else gather_shards,
        mesh=mesh,
        in_specs=(
            P("dp", "groups", "tensor"),
            P("dp", "groups", "tensor"),
            P(("groups", "dp")),
            P(None, "groups", "dp"),
            P("dp", "groups", "tensor"),
        ),
        out_specs=P("dp", "groups"),
        check_vma=False,
    )
```

```python
import math

import jax
import jax.numpy as jnp
from jax import lax
from jax.sharding import PartitionSpec as P

RANK = 32

EDGE = [(0, 1), (1, 0), (2, 3), (3, 2)]
INWARD = [(0, 1), (3, 2)]
OUTWARD = [(1, 0), (2, 3)]
MIDDLE = [(1, 2), (2, 1)]

SCHEDULE = [
    ("exL", ()),
    ("exY", ("grad",)),
    ("mmL", ()),
    ("a2a", ("act", "mmL")),
    ("mmY", ()),
    ("inX", ("act", "exL")),
    ("mmLe", ()),
    ("outLf", ("mmY", "mmL", "x")),
    ("outLm", ("exL", "x")),
    ("core", ("exY", "inX", "a2a")),
    ("mmX", ("exY", "exL", "mmL")),
    ("outYm", ("outLm", "a2a", "y")),
    ("mmY1e", ("inX", "mmLe", "x")),
    ("lanes", ("outLm", "mmX", "mmY1e")),
    ("outY1f", ("outYm", "core", "outLm")),
    ("inG", ("exY", "a2a", "mmLe")),
    ("inLeft", ("a2a", "outLf", "grad")),
    ("mmY2e", ("mmX", "outLf", "outLm")),
    ("outY2f", ("mmY2e", "mmLe", "core")),
    ("mmXe", ("core", "mmY1e")),
]
CUT1, CUT2 = 11, 31


def after(value, *earlier):
    return lax.optimization_barrier((value, *earlier))[0]


def swap(value, distance):
    lanes = lax.axis_size("tensor")
    return lax.ppermute(value, "tensor", [(k, k ^ distance) for k in range(lanes)])


def dot_t(a, b):
    return lax.dot_general(a, b, (((1,), (1,)), ((), ())), preferred_element_type=jnp.float32)


def line_shards(activations, out_grads, lengths, query_left, query_right):
    seq_len = activations.shape[1]
    act = activations.reshape(seq_len, activations.shape[2])
    grad = out_grads.reshape(seq_len, out_grads.shape[2])
    rank_count = RANK
    query_count = query_left.shape[1]
    lanes = lax.axis_size("tensor")
    node = lax.axis_index("dp")
    lane = lax.axis_index("tensor")
    left_rows = query_left.reshape(rank_count * query_count, query_left.shape[2])
    block = query_right.shape[0] * query_count
    right_rows = query_right.reshape(block, query_right.shape[2])
    unit = right_rows.shape[1] // 56
    cut1, cut2 = CUT1 * unit, CUT2 * unit
    share = left_rows.shape[1] // lanes
    third = jnp.where(node < 2, 2, 1)
    fourth = jnp.where(node < 2, 3, 0)
    order = (node, node ^ 1, third, fourth)

    got = {
        "left": lax.dynamic_slice_in_dim(left_rows, lane * share, share, 1),
        "y": right_rows[:, :cut2],
        "x": right_rows[:, cut2:],
        "grad": grad[:, cut2:],
        "act": jnp.stack([act[:, k * share : (k + 1) * share] for k in range(lanes)]),
    }

    def left_partial():
        lefts = (
            got["left"],
            got["exL"],
            got["mmL"] + got["outLm"],
            got["mmLe"] + got["outLf"],
        )
        total = 0.0
        for position, rows in zip(order, lefts):
            own_act = lax.dynamic_index_in_dim(got["a2a"], position, 0, keepdims=False)
            total = total + dot_t(own_act, rows)
        got["partial"] = total
        return total

    def left_pair():
        got["pair"] = got["partial"] + got["core"]
        return got["pair"]

    def left_masked():
        rows = lax.broadcasted_iota(jnp.int32, (seq_len, 1), 0)
        valid = (rows < lengths[0]).astype(jnp.float32)
        got["masked"] = (got["pair"] + got["lanes"]) * valid
        return got["masked"]

    operands = {
        "exL": (lambda: got["left"], EDGE),
        "mmL": (lambda: got["left"], MIDDLE),
        "exY": (lambda: got["y"], EDGE),
        "mmY": (lambda: got["y"], MIDDLE),
        "a2a": (lambda: got["act"], None),
        "mmLe": (lambda: got["exL"], MIDDLE),
        "outLm": (lambda: got["mmL"], OUTWARD),
        "inX": (lambda: got["x"], INWARD),
        "mmX": (lambda: got["x"], MIDDLE),
        "outLf": (lambda: got["mmLe"], OUTWARD),
        "inG": (lambda: got["grad"], INWARD),
        "mmY1e": (lambda: got["exY"][:, :cut1], MIDDLE),
        "outYm": (lambda: got["mmY"], OUTWARD),
        "core": (left_partial, 1),
        "lanes": (left_pair, 2),
        "mmY2e": (lambda: got["exY"][:, cut1:], MIDDLE),
        "outY1f": (lambda: got["mmY1e"], OUTWARD),
        "mmXe": (lambda: got["inX"], MIDDLE),
        "inLeft": (left_masked, INWARD),
        "outY2f": (lambda: got["mmY2e"], OUTWARD),
    }
    for name, waits in SCHEDULE:
        make, route = operands[name]
        value = make()
        if waits:
            value = after(value, *[got[other] for other in waits])
        if route is None:
            got[name] = lax.all_to_all(value, "tensor", 0, 0, tiled=True)
        elif isinstance(route, int):
            got[name] = swap(value, route)
        else:
            got[name] = lax.ppermute(value, "dp", route)

    left, left_end = got["masked"], got["inLeft"]
    is_mid = jnp.logical_or(node == 1, node == 2).astype(jnp.float32)
    columns = [lax.dynamic_slice_in_dim(left, p * block, block, 1) for p in order]
    columns_end = [lax.dynamic_slice_in_dim(left_end, p * block, block, 1) for p in order]
    xs = (got["x"], got["inX"], got["mmX"])
    ys = (got["y"], got["exY"], got["mmY"] + got["outYm"])
    early = [
        dot_t(grad[:, :cut2], y) + is_mid * dot_t(got["grad"], x) for x, y in zip(xs, ys)
    ]
    early.append(dot_t(grad[:, :cut1], got["mmY1e"] + got["outY1f"]))
    early = lax.optimization_barrier(early)
    early_end = lax.optimization_barrier([dot_t(got["inG"], x) for x in xs])
    right_end = early_end + [dot_t(got["inG"], got["mmXe"])]
    end = sum(jnp.sum(c * x, axis=0) for c, x in zip(columns_end, right_end))

    def per_query(value):
        return jnp.sum(value.reshape(block // query_count, query_count), axis=0)[None]

    end = per_query(end)
    grad_own, grad_last = after((got["grad"], grad[:, cut1:cut2]), end)
    end = lax.ppermute(end, "dp", OUTWARD)
    early[3] = early[3] + dot_t(grad_last, got["mmY2e"] + got["outY2f"])
    early[3] = early[3] + is_mid * dot_t(grad_own, got["mmXe"])
    own = sum(jnp.sum(c * y, axis=0) for c, y in zip(columns, early))
    total = (per_query(own) + end) / math.sqrt(seq_len * rank_count)
    total = total + swap(total, 1)
    total = total + swap(total, 2)
    return total


def gather_shards(activations, out_grads, lengths, query_left, query_right):
    seq_len = activations.shape[1]
    act_rows = activations.reshape(seq_len, activations.shape[2])
    grad_rows = out_grads.reshape(seq_len, out_grads.shape[2])
    rank_count = RANK
    query_count = query_left.shape[1]
    shard_piece = lax.all_gather(query_right, "dp", axis=0, tiled=True)
    flat_piece = shard_piece.reshape(shard_piece.shape[0] * query_count, shard_piece.shape[2])
    right_proj = dot_t(grad_rows, flat_piece)
    rank_blocks = lax.all_to_all(query_left, "dp", split_axis=0, concat_axis=2, tiled=True)
    slice_width = act_rows.shape[1]
    offset = lax.axis_index("tensor") * slice_width
    own_columns = lax.dynamic_slice_in_dim(rank_blocks, offset, slice_width, 2)
    shard_piece = lax.all_gather(own_columns, "dp", axis=0, tiled=True)
    flat_piece = shard_piece.reshape(shard_piece.shape[0] * query_count, slice_width)
    left_proj = lax.psum(dot_t(act_rows, flat_piece), "tensor")
    valid_rows = (lax.broadcasted_iota(jnp.int32, (seq_len, 1), 0) < lengths[0]).astype(jnp.float32)
    products = jnp.sum(left_proj * right_proj * valid_rows, axis=0).reshape(rank_count, query_count)
    partial_scores = (jnp.sum(products, axis=0) / math.sqrt(seq_len * rank_count)).reshape(
        1, query_count
    )
    return lax.psum(partial_scores, "tensor")


def solution(mesh):
    line = mesh.shape["dp"] == 4 and mesh.shape["tensor"] == 4
    return jax.shard_map(
        line_shards if line else gather_shards,
        mesh=mesh,
        in_specs=(
            P("dp", "groups", "tensor"),
            P("dp", "groups", "tensor"),
            P(("groups", "dp")),
            P(None, "groups", "dp"),
            P("dp", "groups", "tensor"),
        ),
        out_specs=P("dp", "groups"),
        check_vma=False,
    )
```

```python
import math

import jax
import jax.numpy as jnp
from jax import lax
from jax.sharding import PartitionSpec as P

RANK = 32

EDGE = [(0, 1), (1, 0), (2, 3), (3, 2)]
INWARD = [(0, 1), (3, 2)]
OUTWARD = [(1, 0), (2, 3)]
MIDDLE = [(1, 2), (2, 1)]

SCHEDULE = [
    ("exL", ()),
    ("exY", ("grad",)),
    ("mmL", ()),
    ("a2a", ("act", "mmL")),
    ("mmY", ()),
    ("inX", ("act", "exL")),
    ("mmLe", ()),
    ("outLf", ("mmY", "mmL", "x")),
    ("outLm", ("exL", "x")),
    ("core", ("exY", "inX", "a2a")),
    ("mmX", ("exY", "exL", "mmL")),
    ("outYm", ("outLm", "a2a", "y")),
    ("mmY1e", ("inX", "mmLe", "x")),
    ("lanes", ("outLm", "mmX", "mmY1e")),
    ("outY1f", ("outYm", "core", "outLm")),
    ("inG", ("exY", "a2a", "mmLe")),
    ("inLeft", ("a2a", "outLf", "grad")),
    ("mmY2e", ("mmX", "outLf", "outLm")),
    ("outY2f", ("mmY2e", "mmLe", "core")),
    ("mmXe", ("core", "mmY1e")),
]
CUT1, CUT2 = 13, 30


def after(value, *earlier):
    return lax.optimization_barrier((value, *earlier))[0]


def swap(value, distance):
    lanes = lax.axis_size("tensor")
    return lax.ppermute(value, "tensor", [(k, k ^ distance) for k in range(lanes)])


def dot_t(a, b):
    return lax.dot_general(a, b, (((1,), (1,)), ((), ())), preferred_element_type=jnp.float32)


def line_shards(activations, out_grads, lengths, query_left, query_right):
    seq_len = activations.shape[1]
    act = activations.reshape(seq_len, activations.shape[2])
    grad = out_grads.reshape(seq_len, out_grads.shape[2])
    rank_count = RANK
    query_count = query_left.shape[1]
    lanes = lax.axis_size("tensor")
    node = lax.axis_index("dp")
    lane = lax.axis_index("tensor")
    left_rows = query_left.reshape(rank_count * query_count, query_left.shape[2])
    block = query_right.shape[0] * query_count
    right_rows = query_right.reshape(block, query_right.shape[2])
    unit = right_rows.shape[1] // 56
    cut1, cut2 = CUT1 * unit, CUT2 * unit
    share = left_rows.shape[1] // lanes
    third = jnp.where(node < 2, 2, 1)
    fourth = jnp.where(node < 2, 3, 0)
    order = (node, node ^ 1, third, fourth)

    got = {
        "left": lax.dynamic_slice_in_dim(left_rows, lane * share, share, 1),
        "y": right_rows[:, :cut2],
        "x": right_rows[:, cut2:],
        "grad": grad[:, cut2:],
        "act": jnp.stack([act[:, k * share : (k + 1) * share] for k in range(lanes)]),
    }

    def left_partial():
        lefts = (
            got["left"],
            got["exL"],
            got["mmL"] + got["outLm"],
            got["mmLe"] + got["outLf"],
        )
        total = 0.0
        for position, rows in zip(order, lefts):
            own_act = lax.dynamic_index_in_dim(got["a2a"], position, 0, keepdims=False)
            total = total + dot_t(own_act, rows)
        got["partial"] = total
        return total

    def left_pair():
        got["pair"] = got["partial"] + got["core"]
        return got["pair"]

    def left_masked():
        rows = lax.broadcasted_iota(jnp.int32, (seq_len, 1), 0)
        valid = (rows < lengths[0]).astype(jnp.float32)
        got["masked"] = (got["pair"] + got["lanes"]) * valid
        return got["masked"]

    operands = {
        "exL": (lambda: got["left"], EDGE),
        "mmL": (lambda: got["left"], MIDDLE),
        "exY": (lambda: got["y"], EDGE),
        "mmY": (lambda: got["y"], MIDDLE),
        "a2a": (lambda: got["act"], None),
        "mmLe": (lambda: got["exL"], MIDDLE),
        "outLm": (lambda: got["mmL"], OUTWARD),
        "inX": (lambda: got["x"], INWARD),
        "mmX": (lambda: got["x"], MIDDLE),
        "outLf": (lambda: got["mmLe"], OUTWARD),
        "inG": (lambda: got["grad"], INWARD),
        "mmY1e": (lambda: got["exY"][:, :cut1], MIDDLE),
        "outYm": (lambda: got["mmY"], OUTWARD),
        "core": (left_partial, 1),
        "lanes": (left_pair, 2),
        "mmY2e": (lambda: got["exY"][:, cut1:], MIDDLE),
        "outY1f": (lambda: got["mmY1e"], OUTWARD),
        "mmXe": (lambda: got["inX"], MIDDLE),
        "inLeft": (left_masked, INWARD),
        "outY2f": (lambda: got["mmY2e"], OUTWARD),
    }
    for name, waits in SCHEDULE:
        make, route = operands[name]
        value = make()
        if waits:
            value = after(value, *[got[other] for other in waits])
        if route is None:
            got[name] = lax.all_to_all(value, "tensor", 0, 0, tiled=True)
        elif isinstance(route, int):
            got[name] = swap(value, route)
        else:
            got[name] = lax.ppermute(value, "dp", route)

    left, left_end = got["masked"], got["inLeft"]
    is_mid = jnp.logical_or(node == 1, node == 2).astype(jnp.float32)
    columns = [lax.dynamic_slice_in_dim(left, p * block, block, 1) for p in order]
    columns_end = [lax.dynamic_slice_in_dim(left_end, p * block, block, 1) for p in order]
    xs = (got["x"], got["inX"], got["mmX"])
    ys = (got["y"], got["exY"], got["mmY"] + got["outYm"])
    early = [
        dot_t(grad[:, :cut2], y) + is_mid * dot_t(got["grad"], x) for x, y in zip(xs, ys)
    ]
    early.append(dot_t(grad[:, :cut1], got["mmY1e"] + got["outY1f"]))
    early = lax.optimization_barrier(early)
    early_end = lax.optimization_barrier([dot_t(got["inG"], x) for x in xs])
    right_end = early_end + [dot_t(got["inG"], got["mmXe"])]
    end = sum(jnp.sum(c * x, axis=0) for c, x in zip(columns_end, right_end))

    def per_query(value):
        return jnp.sum(value.reshape(block // query_count, query_count), axis=0)[None]

    end = per_query(end)
    grad_own, grad_last = after((got["grad"], grad[:, cut1:cut2]), end)
    end = lax.ppermute(end, "dp", OUTWARD)
    early[3] = early[3] + dot_t(grad_last, got["mmY2e"] + got["outY2f"])
    early[3] = early[3] + is_mid * dot_t(grad_own, got["mmXe"])
    own = sum(jnp.sum(c * y, axis=0) for c, y in zip(columns, early))
    total = (per_query(own) + end) / math.sqrt(seq_len * rank_count)
    total = total + swap(total, 1)
    total = total + swap(total, 2)
    return total


def gather_shards(activations, out_grads, lengths, query_left, query_right):
    seq_len = activations.shape[1]
    act_rows = activations.reshape(seq_len, activations.shape[2])
    grad_rows = out_grads.reshape(seq_len, out_grads.shape[2])
    rank_count = RANK
    query_count = query_left.shape[1]
    shard_piece = lax.all_gather(query_right, "dp", axis=0, tiled=True)
    flat_piece = shard_piece.reshape(shard_piece.shape[0] * query_count, shard_piece.shape[2])
    right_proj = dot_t(grad_rows, flat_piece)
    rank_blocks = lax.all_to_all(query_left, "dp", split_axis=0, concat_axis=2, tiled=True)
    slice_width = act_rows.shape[1]
    offset = lax.axis_index("tensor") * slice_width
    own_columns = lax.dynamic_slice_in_dim(rank_blocks, offset, slice_width, 2)
    shard_piece = lax.all_gather(own_columns, "dp", axis=0, tiled=True)
    flat_piece = shard_piece.reshape(shard_piece.shape[0] * query_count, slice_width)
    left_proj = lax.psum(dot_t(act_rows, flat_piece), "tensor")
    valid_rows = (lax.broadcasted_iota(jnp.int32, (seq_len, 1), 0) < lengths[0]).astype(jnp.float32)
    products = jnp.sum(left_proj * right_proj * valid_rows, axis=0).reshape(rank_count, query_count)
    partial_scores = (jnp.sum(products, axis=0) / math.sqrt(seq_len * rank_count)).reshape(
        1, query_count
    )
    return lax.psum(partial_scores, "tensor")


def solution(mesh):
    line = mesh.shape["dp"] == 4 and mesh.shape["tensor"] == 4
    return jax.shard_map(
        line_shards if line else gather_shards,
        mesh=mesh,
        in_specs=(
            P("dp", "groups", "tensor"),
            P("dp", "groups", "tensor"),
            P(("groups", "dp")),
            P(None, "groups", "dp"),
            P("dp", "groups", "tensor"),
        ),
        out_specs=P("dp", "groups"),
        check_vma=False,
    )
```
